32 devices in a mesh: section: 4 (over x, core), fsdp: 8 (over z, y).
Axes of the slice: x: 2, y: 2, z: 4, core: 2. Of those that a mesh axis runs over, the one named last changes fastest.
Arguments:
- produced: bfloat16 [4, 24, 256, 4096], P('section', 'fsdp'), may hold values from -6 to 6
- lengths: int32 [4, 24], P('section', 'fsdp'), may hold values from 64 to 256, as said below
- active: int32 [4, 24, 4], P('section', 'fsdp'), may hold values from 0 to 7, all different within a row
- window_blocks: int32 [8], replicated, may hold values from 0 to 249, as said below
- triplets: int32 [4, 8, 3], P('section'), may hold values from 0 to 23, as said below
- teacher: float32 [4, 8], P('section'), may hold values from -60 to 60
- norm_gain: bfloat16 [4096], P('fsdp'), may hold values from 0.5 to 1.5
- head: bfloat16 [32000, 4096], P(None, 'fsdp'), may hold values from -0.09375 to 0.09375
Outputs:
- losses: float32 [4], P('section')
- produced_grad: bfloat16 [4, 24, 256, 4096], P('section', 'fsdp')
- head_grad: float32 [1024, 4096], P(None, 'fsdp')
- gain_grad: float32 [4096], P('fsdp')
The draws below stay inside these ranges and needn't reach their ends.
Inputs may be any that keep to these rules, and one draw needn't show every extreme that they name: `lengths`: every device's first sequence holds 256 tokens, and some sequence holds 64. `active`: each row names 4 different slots. `window_blocks`: ids are distinct. `triplets`: each sequence of a group stands in exactly one triplet, once.
All inputs are finite; a program needn't handle non-finite values.
Results may differ from the reference program's by a relative error of at most 0.0051.
Values may be sent and summed in bfloat16 or wider, within the bound.
A program may use at most 192 MiB of HBM per device.

```python
import jax
import jax.numpy as jnp
from jax import lax

D = 4096
VOCAB = 32000
BLOCK = 128
U = 8
K = 4
LEN = 256
SEQ_DEV = 3
SECTIONS = 4
SEQS = 24
TRIPS = 8
NBLOCKS = 250


def draw_lengths(key, part):
    base = jax.random.randint(key, (SECTIONS, SEQS), LEN // 4, LEN + 1)
    index = jnp.arange(SEQS, dtype=jnp.int32)[None, :]
    base = jnp.where(index % SEQ_DEV == 0, LEN, base)
    return jnp.where(index == 1, LEN // 4, base).astype(jnp.int32)


def draw_window_blocks(key, part):
    others = jax.random.permutation(jax.random.fold_in(key, 1), NBLOCKS - 2)[:U - 2].astype(jnp.int32) + 1
    joined = jnp.concatenate([others, jnp.zeros((1,), jnp.int32), jnp.full((1,), NBLOCKS - 1, jnp.int32)])
    return jax.random.permutation(jax.random.fold_in(key, 2), joined).astype(jnp.int32)


def draw_triplets(key, part):
    section_keys = jax.random.split(jax.random.fold_in(key, 3), SECTIONS)
    orders = jax.vmap(lambda single: jax.random.permutation(single, SEQS))(section_keys)
    return orders.reshape(SECTIONS, TRIPS, 3).astype(jnp.int32)


def steps_of(key, shape, pieces, least, high):
    loudness, own = 1.0, jax.random.fold_in(key, 6)
    for dim, shards_of in pieces:
        heights = jnp.exp(jax.random.uniform(jax.random.fold_in(own, dim), (shards_of,), jnp.float32, least / len(pieces), high / len(pieces)))
        loudness = loudness * jnp.repeat(heights, shape[dim] // shards_of).reshape([-1 if axis == dim else 1 for axis in range(len(shape))])
    return loudness


def different_ones(key, rows, number_of, top, lift):
    order = jax.random.permutation(jax.random.fold_in(key, 1), number_of)
    boost = order
    for power in range(3):
        boost = boost * boost // number_of
    boost = boost * lift // number_of
    tickets = jax.random.randint(jax.random.fold_in(key, 2), (rows, number_of), 0, 4096) + boost
    holders = jax.random.permutation(jax.random.fold_in(key, 3), rows)[jnp.arange(number_of) % rows]
    tickets = jnp.where(jnp.arange(rows)[:, None] == holders[None, :], 1 << 14, tickets)
    merit = tickets * number_of + jnp.arange(number_of)
    return lax.top_k(merit.astype(jnp.int32), top)[1].astype(jnp.int32)


def bell_draw(key, shape, scale, bound, shards=(), kind=jnp.bfloat16):
    array = jax.random.normal(key, shape, jnp.float32) * scale
    if len(shards) > 0:
        array = steps_of(key, shape, shards, -0.22, 0.18) * array
    return jnp.clip(array, min=-bound, max=bound).astype(kind)


def setup_inputs(seed: int = 0) -> dict:
    seeds = jax.random.split(jax.random.key(seed), 9)
    produced = bell_draw(seeds[0], (SECTIONS, SEQS, LEN, D), 1.0, 6.0, ((0, 4), (1, 8)))
    lengths = draw_lengths(jax.random.fold_in(seeds[8], 71), 0)
    active = different_ones(seeds[2], SECTIONS * SEQS, U, K, 8192).reshape((SECTIONS, SEQS, K))
    window_blocks = draw_window_blocks(jax.random.fold_in(seeds[8], 71), 0)
    triplets = draw_triplets(jax.random.fold_in(seeds[8], 71), 0)
    teacher = bell_draw(seeds[5], (SECTIONS, TRIPS), 10.0, 60.0, ((0, 4),), jnp.float32)
    norm_gain = jnp.clip(1.0 + 0.1 * jax.random.normal(seeds[6], (D,), jnp.float32), 0.5, 1.5).astype(jnp.bfloat16)
    head = bell_draw(seeds[7], (VOCAB, D), D ** -0.5, 0.09375, ((1, 8),))
    return dict(produced=produced, lengths=lengths, active=active, window_blocks=window_blocks, triplets=triplets, teacher=teacher, norm_gain=norm_gain, head=head)


eps = 1e-05
loss_scale = 256.0

def pool_terms(logits):
    smooth = jax.nn.softplus(logits)
    return (jnp.log1p(smooth), jax.nn.sigmoid(logits) / (1.0 + smooth))

def reference(produced, lengths, active, window_blocks, triplets, teacher, norm_gain, head):
    offsets = jnp.arange(BLOCK, dtype=jnp.int32)
    block_rows = (window_blocks[:, None] * BLOCK + offsets[None, :]).reshape(-1).astype(jnp.int32)
    window = head[block_rows]
    gain32 = norm_gain.astype(jnp.float32)
    head_total = jnp.zeros((U * BLOCK, D), jnp.float32)
    gain_total = jnp.zeros((D,), jnp.float32)
    losses = []
    returned = [None] * SECTIONS
    position = jnp.arange(LEN, dtype=jnp.int32)
    slot_range = jnp.arange(U, dtype=jnp.int32)
    for target in range(SECTIONS):
        source = (target - 1) % SECTIONS
        hidden = produced[source].reshape(SEQS * LEN, D)
        seq_lengths = lengths[source]
        block_slots = active[source]
        widened = hidden.astype(jnp.float32)
        inv_rms = lax.rsqrt(lax.optimization_barrier(jnp.mean(widened * widened, axis=1, keepdims=True)) + eps)
        normed = (widened * inv_rms * gain32).astype(jnp.bfloat16)
        logits = jnp.dot(normed, window.T, preferred_element_type=jnp.float32).reshape(SEQS, LEN, U * BLOCK)
        values, slopes = pool_terms(logits)
        weight = (position[None, :] < seq_lengths[:, None]).astype(jnp.float32) / seq_lengths[:, None].astype(jnp.float32)
        chosen = lax.optimization_barrier(jnp.sum((block_slots[:, :, None] == slot_range[None, None, :]).astype(jnp.float32), axis=1))
        spread = jnp.repeat(chosen, BLOCK, axis=1)
        pooled = lax.optimization_barrier(jnp.sum(weight[:, :, None] * values, axis=1)) * spread
        triplet_rows = triplets[target]
        query_rows = pooled[triplet_rows[:, 0]]
        positive = pooled[triplet_rows[:, 1]]
        negative = pooled[triplet_rows[:, 2]]
        margin = lax.optimization_barrier(jnp.sum(query_rows * (positive - negative), axis=1))
        deviation = margin - teacher[target]
        losses.append(jnp.mean(deviation * deviation))
        grad_margin = loss_scale * 2.0 * deviation / TRIPS
        grad_pooled = jnp.zeros((SEQS, U * BLOCK), jnp.float32)
        grad_pooled = grad_pooled.at[triplet_rows[:, 0]].add(grad_margin[:, None] * (positive - negative))
        grad_pooled = grad_pooled.at[triplet_rows[:, 1]].add(grad_margin[:, None] * query_rows)
        grad_pooled = grad_pooled.at[triplet_rows[:, 2]].add(-(grad_margin[:, None] * query_rows))
        grad_values = grad_pooled * spread
        grad_logits = (weight[:, :, None] * grad_values[:, None, :] * slopes).astype(jnp.bfloat16)
        grad_logits = grad_logits.reshape(SEQS * LEN, U * BLOCK)
        grad_normed = jnp.dot(grad_logits, window, preferred_element_type=jnp.float32)
        head_total = head_total + jnp.dot(grad_logits.T, normed, preferred_element_type=jnp.float32)
        gain_total = gain_total + lax.optimization_barrier(jnp.sum(grad_normed * widened * inv_rms, axis=0))
        scaled = grad_normed * gain32
        grad_tokens = inv_rms * scaled - widened * (inv_rms * inv_rms * inv_rms) * lax.optimization_barrier(jnp.mean(scaled * widened, axis=1, keepdims=True))
        returned[source] = grad_tokens.astype(jnp.bfloat16).reshape(SEQS, LEN, D)
    return (jnp.stack(losses), jnp.stack(returned), head_total, gain_total)
```

```python
import jax
import jax.numpy as jnp
from jax import lax
from jax.sharding import PartitionSpec as P

D = 4096
BLOCK = 128
U = 8
LEN = 256
SEQ_DEV = 3


eps = 1e-05
loss_scale = 256.0


def passed_along(block, axis, distance):
    devices = range(lax.axis_size(axis))
    route = [((i - distance) % len(devices), i) for i in devices]
    return lax.ppermute(block, axis, route)


def pool_terms(logits):
    smooth = jax.nn.softplus(logits)
    return (jnp.log1p(smooth), jax.nn.sigmoid(logits) / (1.0 + smooth))


def local(produced, lengths, active, window_blocks, triplets, teacher, norm_gain, head):
    sections, shards = lax.axis_size("section"), lax.axis_size("fsdp")
    group_data = jnp.concatenate([triplets[0].astype(jnp.float32), teacher[0][:, None]], axis=1)
    group_data = passed_along(group_data, "section", -1)
    triplet_rows = group_data[:, :3].astype(jnp.int32)
    target = group_data[:, 3]
    columns = head.shape[1]
    own_blocks = U // sections
    block_ids = lax.dynamic_slice(
        window_blocks, (lax.axis_index("section") * own_blocks,), (own_blocks,)
    )
    local_rows = head.reshape(head.shape[0] // BLOCK, BLOCK, columns)[block_ids].reshape(
        own_blocks * BLOCK, columns
    )
    piece = lax.all_gather(local_rows, "fsdp", axis=1, tiled=True)
    window = lax.all_gather(piece, "section", axis=0, tiled=True)
    gain_full = lax.all_gather(norm_gain, "fsdp", axis=0, tiled=True)
    gain32 = gain_full.astype(jnp.float32)
    tokens = produced.reshape(SEQ_DEV * LEN, D)
    widened = tokens.astype(jnp.float32)
    inv_rms = lax.rsqrt(jnp.mean(widened * widened, axis=1, keepdims=True) + eps)
    normed = (widened * inv_rms * gain32).astype(jnp.bfloat16)
    seq_len_row = lengths[0]
    slot_table = active[0]
    position = jnp.arange(LEN, dtype=jnp.int32)
    weight = (position[None, :] < seq_len_row[:, None]).astype(jnp.float32) / seq_len_row[
        :, None
    ].astype(jnp.float32)
    slot_range = jnp.arange(U, dtype=jnp.int32)
    onehot = (slot_table[:, :, None] == slot_range[None, None, :]).astype(jnp.float32)
    chosen = jnp.sum(onehot, axis=1)
    spread = jnp.repeat(chosen, BLOCK, axis=1)
    logits = jnp.einsum("td,jd->tj", normed, window, preferred_element_type=jnp.float32)
    values, slopes = pool_terms(logits.reshape(SEQ_DEV, LEN, U * BLOCK))
    pooled = jnp.sum(weight[:, :, None] * values, axis=1) * spread
    all_pooled = lax.all_gather(pooled, "fsdp", axis=0, tiled=True)
    query_rows = all_pooled[triplet_rows[:, 0]]
    positive = all_pooled[triplet_rows[:, 1]]
    negative = all_pooled[triplet_rows[:, 2]]
    margin = jnp.sum(query_rows * (positive - negative), axis=1)
    deviation = margin - target
    loss_value = passed_along(jnp.mean(deviation * deviation).reshape(1), "section", 1)
    grad_margin = loss_scale * 2.0 * deviation / triplets.shape[1]
    first_row = lax.axis_index("fsdp") * SEQ_DEV
    own_rows = first_row + jnp.arange(SEQ_DEV, dtype=jnp.int32)
    query_hits = (triplet_rows[:, 0][:, None] == own_rows[None, :]).astype(jnp.float32)
    positive_hits = (triplet_rows[:, 1][:, None] == own_rows[None, :]).astype(jnp.float32)
    negative_hits = (triplet_rows[:, 2][:, None] == own_rows[None, :]).astype(jnp.float32)
    query_term = grad_margin[:, None] * (positive - negative)
    other_term = grad_margin[:, None] * query_rows
    grad_pooled = jnp.einsum("ts,tj->sj", query_hits, query_term, precision=lax.Precision.HIGHEST)
    grad_pooled = grad_pooled + jnp.einsum(
        "ts,tj->sj", positive_hits - negative_hits, other_term, precision=lax.Precision.HIGHEST
    )
    grad_values = grad_pooled * spread
    grad_logits = (weight[:, :, None] * grad_values[:, None, :] * slopes).astype(jnp.bfloat16)
    grad_logits = grad_logits.reshape(SEQ_DEV * LEN, U * BLOCK)
    head_part = jnp.einsum(
        "tj,td->jd", grad_logits, normed, preferred_element_type=jnp.float32
    ).astype(jnp.bfloat16)
    rows = U * BLOCK // sections
    parts = lax.all_to_all(
        head_part.reshape(sections, rows, D), "section", split_axis=0, concat_axis=0
    )
    mine = jnp.sum(parts.astype(jnp.float32), axis=0).astype(jnp.bfloat16)
    parts = lax.all_to_all(
        mine.reshape(rows, shards, columns), "fsdp", split_axis=1, concat_axis=0
    )
    parts = parts.reshape(shards, rows, columns)
    mine = jnp.sum(parts.astype(jnp.float32), axis=0).astype(jnp.bfloat16)
    head_piece = lax.all_gather(mine, "section", axis=0, tiled=True).astype(jnp.float32)
    grad_normed = jnp.dot(grad_logits, window, preferred_element_type=jnp.float32)
    gain_part = jnp.sum(grad_normed * widened * inv_rms, axis=0)
    scaled = grad_normed * gain32
    grad_tokens = inv_rms * scaled - widened * (inv_rms * inv_rms * inv_rms) * jnp.mean(
        scaled * widened, axis=1, keepdims=True
    )
    outgoing = grad_tokens.astype(jnp.bfloat16).reshape(1, SEQ_DEV, LEN, D)
    gain_piece = lax.psum_scatter(gain_part, "fsdp", scatter_dimension=0, tiled=True)
    gain_piece = lax.psum(gain_piece, "section")
    return (loss_value, outgoing, head_piece, gain_piece)


def solution(mesh):
    return jax.shard_map(
        local,
        mesh=mesh,
        in_specs=(
            P("section", "fsdp", None, None),
            P("section", "fsdp"),
            P("section", "fsdp", None),
            P(),
            P("section", None, None),
            P("section", None),
            P("fsdp"),
            P(None, "fsdp"),
        ),
        out_specs=(P("section"), P("section", "fsdp", None, None), P(None, "fsdp"), P("fsdp")),
        check_vma=False,
    )
```

```python
import jax
import jax.numpy as jnp
from jax import lax
from jax.experimental import pallas as pl
from jax.experimental.pallas import tpu as pltpu
from jax.sharding import PartitionSpec as P

D = 4096
BLOCK = 128
U = 8
LEN = 256
SEQ_DEV = 3


eps = 1e-05
loss_scale = 256.0


def passed_along(block, axis, distance):
    devices = range(lax.axis_size(axis))
    route = [((i - distance) % len(devices), i) for i in devices]
    return lax.ppermute(block, axis, route)


def pool_terms(logits):
    smooth = jax.nn.softplus(logits)
    return (jnp.log1p(smooth), jax.nn.sigmoid(logits) / (1.0 + smooth))


MESH = pl.DeviceIdType.MESH
VMEM = pl.BlockSpec(memory_space=pltpu.VMEM)
ANY = pl.BlockSpec(memory_space=pl.ANY)
bf16, f32 = jnp.bfloat16, jnp.float32


def place():
    s, f = lax.axis_index("section"), lax.axis_index("fsdp")
    mate = s + 1 - 2 * lax.rem(s, 2)
    across = lax.rem(s + 2, 4)
    return s, f, mate, across


def greet(others):
    barrier = pltpu.get_barrier_semaphore()
    for device in others:
        pl.semaphore_signal(barrier, inc=1, device_id=device, device_id_type=MESH)
    pl.semaphore_wait(barrier, len(others))


def remote(src, dst, send, recv, device):
    return pltpu.make_async_remote_copy(
        src_ref=src,
        dst_ref=dst,
        send_sem=send,
        recv_sem=recv,
        device_id=device,
        device_id_type=MESH,
    )


def gather_kernel(n, piece_ref, gain_ref, window_ref, gains_ref, send, recv, gsend, grecv, own_sem):
    s, f, mate, across = place()
    lines = n // 2
    a, b = lax.div(f, 2), lax.rem(f, 2)
    rows, columns = piece_ref.shape
    peers = [(s, lax.rem(f + d, n)) for d in range(1, n)]
    greet(peers + [(mate, f), (across, f)])
    sent = []

    def region(q, g):
        return window_ref.at[
            pl.ds(pl.multiple_of(q * rows, rows), rows),
            pl.ds(pl.multiple_of(g * columns, columns), columns),
        ]

    def push(src, q, g, index, device):
        copy = remote(src, region(q, g), send.at[index], recv.at[index], device)
        copy.start()
        sent.append(copy)

    def arrive(q, g, index):
        spot = region(q, g)
        remote(spot, spot, send.at[index], recv.at[index], (mate, f)).wait_recv()
        return spot

    side = lambda d: 2 * lax.rem(a - d + lines, lines) + b
    other = lambda d: 2 * lax.rem(a - d + lines, lines) + 1 - b
    to_y, to_x, to_mate, to_last = lines, 2 * lines, 4 * lines, 6 * lines

    def spread_out(src, g, d, half):
        push(src, s, g, to_x + half * lines + d, (across, f))
        push(src, s, g, to_mate + half * lines + d, (mate, f))

    for d in range(1, lines):
        push(piece_ref, s, f, d, (s, 2 * lax.rem(a + d, lines) + b))
    push(piece_ref, s, f, to_y, (s, 2 * a + 1 - b))
    spread_out(piece_ref, f, 0, 0)
    own = pltpu.make_async_copy(piece_ref, region(s, f), own_sem)
    own.start()
    gain_copies = []
    for d in range(1, n):
        copy = remote(gain_ref, gains_ref.at[f], gsend.at[d], grecv.at[d], peers[d - 1])
        copy.start()
        gain_copies.append(copy)
    gains_ref[f] = gain_ref[...]
    spread_out(arrive(s, other(0), to_y), other(0), 0, 1)
    for d in range(1, lines):
        spot = arrive(s, side(d), d)
        push(spot, s, side(d), to_y + d, (s, 2 * a + 1 - b))
        spread_out(spot, side(d), d, 0)
    for d in range(1, lines):
        spread_out(arrive(s, other(d), to_y + d), other(d), d, 1)
    order = [(0, 0), (0, 1)] + [(d, 0) for d in range(1, lines)] + [(d, 1) for d in range(1, lines)]
    name = lambda d, half: other(d) if half else side(d)
    for d, half in order:
        spot = arrive(across, name(d, half), to_x + half * lines + d)
        push(spot, across, name(d, half), to_last + half * lines + d, (mate, f))
    mate_across = lax.rem(mate + 2, 4)
    for d, half in order:
        arrive(mate, name(d, half), to_mate + half * lines + d)
        arrive(mate_across, name(d, half), to_last + half * lines + d)
    for d in range(1, n):
        spot = gains_ref.at[lax.rem(f - d + n, n)]
        remote(spot, spot, gsend.at[d], grecv.at[d], peers[d - 1]).wait_recv()
    own.wait()
    for copy in sent + gain_copies:
        copy.wait_send()


def gather_window(piece, gain, n):
    rows, columns = piece.shape
    count = 8 * (n // 2)
    return pl.pallas_call(
        lambda *refs: gather_kernel(n, *refs),
        name="gather_window",
        out_shape=(
            jax.ShapeDtypeStruct((4 * rows, n * columns), bf16),
            jax.ShapeDtypeStruct((n, 1, columns), f32),
        ),
        in_specs=[VMEM, VMEM],
        out_specs=(ANY, VMEM),
        scratch_shapes=[
            pltpu.SemaphoreType.DMA((count,)),
            pltpu.SemaphoreType.DMA((count,)),
            pltpu.SemaphoreType.DMA((n,)),
            pltpu.SemaphoreType.DMA((n,)),
            pltpu.SemaphoreType.DMA,
        ],
        compiler_params=pltpu.CompilerParams(collective_id=0, has_side_effects=True),
    )(piece, gain)


def pool_kernel(n, in_ref, out_ref, send, recv):
    s, f, _, _ = place()
    peers = [(s, lax.rem(f + d, n)) for d in range(1, n)]
    greet(peers)
    copies = []
    for d in range(1, n):
        copy = remote(in_ref, out_ref.at[f], send.at[d], recv.at[d], peers[d - 1])
        copy.start()
        copies.append(copy)
    out_ref[f] = in_ref[...]
    for d in range(1, n):
        spot = out_ref.at[lax.rem(f - d + n, n)]
        remote(spot, spot, send.at[d], recv.at[d], peers[d - 1]).wait_recv()
    for copy in copies:
        copy.wait_send()


def gather_pooled(pooled, n):
    return pl.pallas_call(
        lambda *refs: pool_kernel(n, *refs),
        name="gather_pooled",
        out_shape=jax.ShapeDtypeStruct((n,) + pooled.shape, f32),
        in_specs=[VMEM],
        out_specs=VMEM,
        scratch_shapes=[pltpu.SemaphoreType.DMA((n,)), pltpu.SemaphoreType.DMA((n,))],
        compiler_params=pltpu.CompilerParams(collective_id=1, has_side_effects=True),
    )(pooled)


def reduce_kernel(
    n, part_ref, gain_ref, out_ref, gain_out,
    got_mate, sum_x, got_x, sum_y, got_y, sum_z, got_z, final, got_gain, gain_sum, got_sum,
    send_a, recv_a, send_x, recv_x, send_y, recv_y, send_z, recv_z, send_o, recv_o,
    gsend, grecv, ssend, srecv,
):
    s, f, mate, across = place()
    lines = n // 2
    a, b = lax.div(f, 2), lax.rem(f, 2)
    rows, columns = final.shape
    diagonal = lax.rem(mate + 2, 4)
    peers = [(s, lax.rem(f + d, n)) for d in range(1, n)]
    sections = [(lax.rem(s + d, 4), f) for d in range(1, 4)]
    greet(peers + sections)
    sent = []

    def push(src, dst, send, recv, device):
        copy = remote(src, dst, send, recv, device)
        copy.start()
        sent.append(copy)

    def arrive(spot, send, recv):
        remote(spot, spot, send, recv, (mate, f)).wait_recv()

    chunk = [lax.rem(a + 1 + d, lines) for d in range(lines)]

    def band(q):
        return pl.ds(pl.multiple_of(q * rows, rows), rows)

    def span(d):
        return pl.ds(pl.multiple_of(chunk[d] * 2 * columns, 2 * columns), 2 * columns)

    def half_span(d, half):
        return pl.ds(
            pl.multiple_of((chunk[d] * 2 + half) * columns, columns), columns
        )

    def half(h):
        return pl.ds(pl.multiple_of(h * columns, columns), columns)

    for d in range(lines):
        for k, q in ((0, diagonal), (1, mate)):
            push(
                part_ref.at[band(q), span(d)], got_mate.at[d, k],
                send_a.at[d, k], recv_a.at[d, k], (mate, f),
            )
    for d in range(1, n):
        device = peers[d - 1]
        push(gain_ref.at[device[1]], got_gain.at[d], gsend.at[d], grecv.at[d], device)
    for d in range(lines):
        arrive(got_mate.at[d, 0], send_a.at[d, 0], recv_a.at[d, 0])
        sum_x[d] = (
            part_ref[band(across), span(d)].astype(f32) + got_mate[d, 0].astype(f32)
        ).astype(bf16)
        push(sum_x.at[d], got_x.at[d], send_x.at[d], recv_x.at[d], (across, f))
    total = gain_ref[f]
    for d in range(1, n):
        arrive(got_gain.at[d], gsend.at[d], grecv.at[d])
        total = total + got_gain[d]
    gain_sum[...] = total
    for d in range(1, 4):
        push(gain_sum, got_sum.at[d], ssend.at[d], srecv.at[d], sections[d - 1])

    def gathered(d, h):
        return (
            part_ref[band(s), half_span(d, h)].astype(f32)
            + got_mate[d, 1, :, half(h)].astype(f32)
            + got_x[d, :, half(h)].astype(f32)
        )

    def finish(d):
        arrive(got_y.at[d], send_y.at[d], recv_y.at[d])
        value = gathered(d, b) + got_y[d].astype(f32)
        if d < lines - 1:
            sum_z[d] = value.astype(bf16)
            push(sum_z.at[d], got_z.at[d], send_z.at[d], recv_z.at[d], (s, 2 * chunk[d] + b))
        return value

    for d in range(lines):
        arrive(got_mate.at[d, 1], send_a.at[d, 1], recv_a.at[d, 1])
        arrive(got_x.at[d], send_x.at[d], recv_x.at[d])
        sum_y[d] = gathered(d, 1 - b).astype(bf16)
        push(sum_y.at[d], got_y.at[d], send_y.at[d], recv_y.at[d], (s, 2 * a + 1 - b))
        if d > 0:
            finish(d - 1)
    value = finish(lines - 1)
    for d in range(lines - 1):
        arrive(got_z.at[d], send_z.at[d], recv_z.at[d])
        value = value + got_z[d].astype(f32)
    final[...] = value.astype(bf16)
    push(final, out_ref.at[band(s)], send_o.at[0], recv_o.at[0], (across, f))
    push(final, out_ref.at[band(s)], send_o.at[1], recv_o.at[1], (mate, f))
    out_ref[band(s), :] = value.astype(bf16)
    for d in range(1, 4):
        arrive(got_sum.at[d], ssend.at[d], srecv.at[d])
    gain_out[...] = gain_sum[...] + got_sum[1] + got_sum[2] + got_sum[3]
    arrive(out_ref.at[band(across)], send_o.at[0], recv_o.at[0])
    push(
        out_ref.at[band(across)], out_ref.at[band(across)],
        send_o.at[2], recv_o.at[2], (mate, f),
    )
    arrive(out_ref.at[band(mate)], send_o.at[1], recv_o.at[1])
    arrive(out_ref.at[band(diagonal)], send_o.at[2], recv_o.at[2])
    for copy in sent:
        copy.wait_send()


def reduce_head(part, gain, n):
    terms, width = part.shape
    rows, columns, lines = terms // 4, width // n, n // 2
    sems = [pltpu.SemaphoreType.DMA((lines, 2))] * 2 + [pltpu.SemaphoreType.DMA((lines,))] * 6
    sems += [pltpu.SemaphoreType.DMA((3,))] * 2 + [pltpu.SemaphoreType.DMA((n,))] * 2
    sems += [pltpu.SemaphoreType.DMA((4,))] * 2
    return pl.pallas_call(
        lambda *refs: reduce_kernel(n, *refs),
        name="reduce_head",
        out_shape=(
            jax.ShapeDtypeStruct((terms, columns), bf16),
            jax.ShapeDtypeStruct((1, columns), f32),
        ),
        in_specs=[VMEM, VMEM],
        out_specs=(VMEM, VMEM),
        scratch_shapes=[
            pltpu.VMEM((lines, 2, rows, 2 * columns), bf16),
            pltpu.VMEM((lines, rows, 2 * columns), bf16),
            pltpu.VMEM((lines, rows, 2 * columns), bf16),
            pltpu.VMEM((lines, rows, columns), bf16),
            pltpu.VMEM((lines, rows, columns), bf16),
            pltpu.VMEM((lines, rows, columns), bf16),
            pltpu.VMEM((lines, rows, columns), bf16),
            pltpu.VMEM((rows, columns), bf16),
            pltpu.VMEM((n, 1, columns), f32),
            pltpu.VMEM((1, columns), f32),
            pltpu.VMEM((4, 1, columns), f32),
        ]
        + sems,
        compiler_params=pltpu.CompilerParams(
            collective_id=2, has_side_effects=True, vmem_limit_bytes=56 << 20
        ),
    )(part, gain)


def local(produced, lengths, active, window_blocks, triplets, teacher, norm_gain, head):
    sections, shards = lax.axis_size("section"), lax.axis_size("fsdp")
    group_data = jnp.concatenate([triplets[0].astype(jnp.float32), teacher[0][:, None]], axis=1)
    group_data = passed_along(group_data, "section", -1)
    triplet_rows = group_data[:, :3].astype(jnp.int32)
    target = group_data[:, 3]
    columns = head.shape[1]
    own_blocks = U // sections
    block_ids = lax.dynamic_slice(
        window_blocks, (lax.axis_index("section") * own_blocks,), (own_blocks,)
    )
    local_rows = head.reshape(head.shape[0] // BLOCK, BLOCK, columns)[block_ids].reshape(
        own_blocks * BLOCK, columns
    )
    gain_own = norm_gain.astype(jnp.float32)[None, :]
    window, gains = gather_window(local_rows, gain_own, shards)
    gain32 = gains.reshape(D)
    tokens = produced.reshape(SEQ_DEV * LEN, D)
    widened = tokens.astype(jnp.float32)
    inv_rms = lax.rsqrt(jnp.mean(widened * widened, axis=1, keepdims=True) + eps)
    normed = (widened * inv_rms * gain32).astype(jnp.bfloat16)
    seq_len_row = lengths[0]
    slot_table = active[0]
    position = jnp.arange(LEN, dtype=jnp.int32)
    weight = (position[None, :] < seq_len_row[:, None]).astype(jnp.float32) / seq_len_row[
        :, None
    ].astype(jnp.float32)
    slot_range = jnp.arange(U, dtype=jnp.int32)
    onehot = (slot_table[:, :, None] == slot_range[None, None, :]).astype(jnp.float32)
    chosen = jnp.sum(onehot, axis=1)
    spread = jnp.repeat(chosen, BLOCK, axis=1)
    logits = jnp.einsum("td,jd->tj", normed, window, preferred_element_type=jnp.float32)
    values, slopes = pool_terms(logits.reshape(SEQ_DEV, LEN, U * BLOCK))
    pooled = jnp.sum(weight[:, :, None] * values, axis=1) * spread
    all_pooled = gather_pooled(pooled, shards).reshape(shards * SEQ_DEV, U * BLOCK)
    query_rows = all_pooled[triplet_rows[:, 0]]
    positive = all_pooled[triplet_rows[:, 1]]
    negative = all_pooled[triplet_rows[:, 2]]
    margin = jnp.sum(query_rows * (positive - negative), axis=1)
    deviation = margin - target
    loss_value = passed_along(jnp.mean(deviation * deviation).reshape(1), "section", 1)
    grad_margin = loss_scale * 2.0 * deviation / triplets.shape[1]
    first_row = lax.axis_index("fsdp") * SEQ_DEV
    own_rows = first_row + jnp.arange(SEQ_DEV, dtype=jnp.int32)
    query_hits = (triplet_rows[:, 0][:, None] == own_rows[None, :]).astype(jnp.float32)
    positive_hits = (triplet_rows[:, 1][:, None] == own_rows[None, :]).astype(jnp.float32)
    negative_hits = (triplet_rows[:, 2][:, None] == own_rows[None, :]).astype(jnp.float32)
    query_term = grad_margin[:, None] * (positive - negative)
    other_term = grad_margin[:, None] * query_rows
    grad_pooled = jnp.einsum("ts,tj->sj", query_hits, query_term, precision=lax.Precision.HIGHEST)
    grad_pooled = grad_pooled + jnp.einsum(
        "ts,tj->sj", positive_hits - negative_hits, other_term, precision=lax.Precision.HIGHEST
    )
    grad_values = grad_pooled * spread
    grad_logits = (weight[:, :, None] * grad_values[:, None, :] * slopes).astype(jnp.bfloat16)
    grad_logits = grad_logits.reshape(SEQ_DEV * LEN, U * BLOCK)
    head_part = jnp.einsum(
        "tj,td->jd", grad_logits, normed, preferred_element_type=jnp.float32
    ).astype(jnp.bfloat16)
    grad_normed = jnp.dot(grad_logits, window, preferred_element_type=jnp.float32)
    gain_part = jnp.sum(grad_normed * widened * inv_rms, axis=0)
    scaled = grad_normed * gain32
    grad_tokens = inv_rms * scaled - widened * (inv_rms * inv_rms * inv_rms) * jnp.mean(
        scaled * widened, axis=1, keepdims=True
    )
    outgoing = grad_tokens.astype(jnp.bfloat16).reshape(1, SEQ_DEV, LEN, D)
    head_piece, gain_piece = reduce_head(head_part, gain_part.reshape(shards, 1, columns), shards)
    head_piece = head_piece.astype(jnp.float32)
    gain_piece = gain_piece.reshape(columns)
    return (loss_value, outgoing, head_piece, gain_piece)


def solution(mesh):
    return jax.shard_map(
        local,
        mesh=mesh,
        in_specs=(
            P("section", "fsdp", None, None),
            P("section", "fsdp"),
            P("section", "fsdp", None),
            P(),
            P("section", None, None),
            P("section", None),
            P("fsdp"),
            P(None, "fsdp"),
        ),
        out_specs=(P("section"), P("section", "fsdp", None, None), P(None, "fsdp"), P("fsdp")),
        check_vma=False,
    )
```

```python
import jax
import jax.numpy as jnp
from jax import lax
from jax.experimental import pallas as pl
from jax.experimental.pallas import tpu as pltpu
from jax.sharding import PartitionSpec as P

D = 4096
BLOCK = 128
U = 8
LEN = 256
SEQ_DEV = 3


eps = 1e-05
loss_scale = 256.0


def passed_along(block, axis, distance):
    devices = range(lax.axis_size(axis))
    route = [((i - distance) % len(devices), i) for i in devices]
    return lax.ppermute(block, axis, route)


def pool_terms(logits):
    smooth = jax.nn.softplus(logits)
    return (jnp.log1p(smooth), jax.nn.sigmoid(logits) / (1.0 + smooth))


MESH = pl.DeviceIdType.MESH
VMEM = pl.BlockSpec(memory_space=pltpu.VMEM)
ANY = pl.BlockSpec(memory_space=pl.ANY)
bf16, f32 = jnp.bfloat16, jnp.float32


def place():
    s, f = lax.axis_index("section"), lax.axis_index("fsdp")
    mate = s + 1 - 2 * lax.rem(s, 2)
    across = lax.rem(s + 2, 4)
    return s, f, mate, across


def greet(others):
    barrier = pltpu.get_barrier_semaphore()
    for device in others:
        pl.semaphore_signal(barrier, inc=1, device_id=device, device_id_type=MESH)
    pl.semaphore_wait(barrier, len(others))


def remote(src, dst, send, recv, device):
    return pltpu.make_async_remote_copy(
        src_ref=src,
        dst_ref=dst,
        send_sem=send,
        recv_sem=recv,
        device_id=device,
        device_id_type=MESH,
    )


def gather_kernel(n, piece_ref, gain_ref, window_ref, gains_ref, send, recv, gsend, grecv, own_sem):
    s, f, mate, across = place()
    lines = n // 2
    a, b = lax.div(f, 2), lax.rem(f, 2)
    rows, columns = piece_ref.shape
    peers = [(s, lax.rem(f + d, n)) for d in range(1, n)]
    greet(peers + [(mate, f), (across, f)])
    sent = []

    def region(q, g):
        return window_ref.at[
            pl.ds(pl.multiple_of(q * rows, rows), rows),
            pl.ds(pl.multiple_of(g * columns, columns), columns),
        ]

    def push(src, q, g, index, device):
        copy = remote(src, region(q, g), send.at[index], recv.at[index], device)
        copy.start()
        sent.append(copy)

    def arrive(q, g, index):
        spot = region(q, g)
        remote(spot, spot, send.at[index], recv.at[index], (mate, f)).wait_recv()
        return spot

    side = lambda d: 2 * lax.rem(a - d + lines, lines) + b
    other = lambda d: 2 * lax.rem(a - d + lines, lines) + 1 - b
    to_y, to_x, to_mate, to_last = lines, 2 * lines, 4 * lines, 6 * lines

    def spread_out(src, g, d, half):
        push(src, s, g, to_x + half * lines + d, (across, f))
        push(src, s, g, to_mate + half * lines + d, (mate, f))

    for d in range(1, lines):
        push(piece_ref, s, f, d, (s, 2 * lax.rem(a + d, lines) + b))
    push(piece_ref, s, f, to_y, (s, 2 * a + 1 - b))
    spread_out(piece_ref, f, 0, 0)
    own = pltpu.make_async_copy(piece_ref, region(s, f), own_sem)
    own.start()
    gain_copies = []
    for d in range(1, n):
        copy = remote(gain_ref, gains_ref.at[f], gsend.at[d], grecv.at[d], peers[d - 1])
        copy.start()
        gain_copies.append(copy)
    gains_ref[f] = gain_ref[...]
    spread_out(arrive(s, other(0), to_y), other(0), 0, 1)
    for d in range(1, lines):
        spot = arrive(s, side(d), d)
        push(spot, s, side(d), to_y + d, (s, 2 * a + 1 - b))
        spread_out(spot, side(d), d, 0)
    for d in range(1, lines):
        spread_out(arrive(s, other(d), to_y + d), other(d), d, 1)
    order = [(0, 0), (0, 1)] + [(d, 0) for d in range(1, lines)] + [(d, 1) for d in range(1, lines)]
    name = lambda d, half: other(d) if half else side(d)
    for d, half in order:
        spot = arrive(across, name(d, half), to_x + half * lines + d)
        push(spot, across, name(d, half), to_last + half * lines + d, (mate, f))
    mate_across = lax.rem(mate + 2, 4)
    for d, half in order:
        arrive(mate, name(d, half), to_mate + half * lines + d)
        arrive(mate_across, name(d, half), to_last + half * lines + d)
    for d in range(1, n):
        spot = gains_ref.at[lax.rem(f - d + n, n)]
        remote(spot, spot, gsend.at[d], grecv.at[d], peers[d - 1]).wait_recv()
    own.wait()
    for copy in sent + gain_copies:
        copy.wait_send()


def gather_window(piece, gain, n):
    rows, columns = piece.shape
    count = 8 * (n // 2)
    return pl.pallas_call(
        lambda *refs: gather_kernel(n, *refs),
        name="gather_window",
        out_shape=(
            jax.ShapeDtypeStruct((4 * rows, n * columns), bf16),
            jax.ShapeDtypeStruct((n, 1, columns), f32),
        ),
        in_specs=[VMEM, VMEM],
        out_specs=(ANY, VMEM),
        scratch_shapes=[
            pltpu.SemaphoreType.DMA((count,)),
            pltpu.SemaphoreType.DMA((count,)),
            pltpu.SemaphoreType.DMA((n,)),
            pltpu.SemaphoreType.DMA((n,)),
            pltpu.SemaphoreType.DMA,
        ],
        compiler_params=pltpu.CompilerParams(collective_id=0, has_side_effects=True),
    )(piece, gain)


PAD = 8


def pick(hits, rows):
    return jnp.dot(hits, rows, precision=lax.Precision.HIGHEST, preferred_element_type=f32)


def pool_kernel(n, in_ref, group_ref, turned_ref, spread_ref, grad_ref, loss_ref, held, send, recv):
    s, f, _, _ = place()
    trips = group_ref.shape[0]
    peers = [(s, lax.rem(f + d, n)) for d in range(1, n)]
    greet(peers)
    copies = []
    for d in range(1, n):
        copy = remote(in_ref, held.at[f], send.at[d], recv.at[d], peers[d - 1])
        copy.start()
        copies.append(copy)
    held[f] = in_ref[...]
    names = lax.broadcasted_iota(jnp.int32, (trips, n * PAD), 1).astype(f32)
    group = group_ref[...]
    hits = [(names == group[:, k : k + 1]).astype(f32) for k in range(3)]
    own = (lax.broadcasted_iota(jnp.int32, (PAD, trips), 0) + f * PAD).astype(f32)
    turned = turned_ref[...]
    own_hits = [(own == turned[k : k + 1, :]).astype(f32) for k in range(3)]
    for d in range(1, n):
        spot = held.at[lax.rem(f - d + n, n)]
        remote(spot, spot, send.at[d], recv.at[d], peers[d - 1]).wait_recv()
    rows = held[...].reshape(n * PAD, held.shape[2])
    query = pick(hits[0], rows)
    gap = pick(hits[1], rows) - pick(hits[2], rows)
    deviation = jnp.sum(query * gap, axis=1, keepdims=True) - group[:, 3:4]
    loss = jnp.sum(deviation * deviation, axis=0, keepdims=True) / trips
    loss_ref[...] = jnp.broadcast_to(loss, loss_ref.shape)
    grad_margin = loss_scale * 2.0 * deviation / trips
    grad = pick(own_hits[0], grad_margin * gap)
    grad = grad + pick(own_hits[1] - own_hits[2], grad_margin * query)
    grad_ref[...] = grad * spread_ref[...]
    for copy in copies:
        copy.wait_send()


def pooled_grads(pooled, group, spread, n):
    return pl.pallas_call(
        lambda *refs: pool_kernel(n, *refs),
        name="pooled_grads",
        out_shape=(
            jax.ShapeDtypeStruct(pooled.shape, f32),
            jax.ShapeDtypeStruct((1, 128), f32),
        ),
        in_specs=[VMEM] * 4,
        out_specs=(VMEM, VMEM),
        scratch_shapes=[
            pltpu.VMEM((n,) + pooled.shape, f32),
            pltpu.SemaphoreType.DMA((n,)),
            pltpu.SemaphoreType.DMA((n,)),
        ],
        compiler_params=pltpu.CompilerParams(collective_id=1, has_side_effects=True),
    )(pooled, group, group.T, spread)


def reduce_kernel(
    n, part_ref, logit_ref, window_hbm, token_hbm, inv_ref, norm_ref, out_ref, gain_out, grad_hbm,
    window_ref, token_ref, grad_ref, product, gain_row, gain_ref, load_sem, store_sem,
    got_mate, sum_x, got_x, sum_y, got_y, sum_z, got_z, final, got_gain, gain_sum, got_sum,
    send_a, recv_a, send_x, recv_x, send_y, recv_y, send_z, recv_z, send_o, recv_o,
    gsend, grecv, ssend, srecv,
):
    s, f, mate, across = place()
    lines = n // 2
    a, b = lax.div(f, 2), lax.rem(f, 2)
    rows, columns = final.shape
    diagonal = lax.rem(mate + 2, 4)
    peers = [(s, lax.rem(f + d, n)) for d in range(1, n)]
    sections = [(lax.rem(s + d, 4), f) for d in range(1, 4)]
    greet(peers + sections)
    sent = []

    def push(src, dst, send, recv, device):
        copy = remote(src, dst, send, recv, device)
        copy.start()
        sent.append(copy)

    def arrive(spot, send, recv):
        remote(spot, spot, send, recv, (mate, f)).wait_recv()

    chunk = [lax.rem(a + 1 + d, lines) for d in range(lines)]

    def band(q):
        return pl.ds(pl.multiple_of(q * rows, rows), rows)

    def span(d):
        return pl.ds(pl.multiple_of(chunk[d] * 2 * columns, 2 * columns), 2 * columns)

    def half_span(d, half):
        return pl.ds(
            pl.multiple_of((chunk[d] * 2 + half) * columns, columns), columns
        )

    def half(h):
        return pl.ds(pl.multiple_of(h * columns, columns), columns)

    for d in range(lines):
        for k, q in ((0, diagonal), (1, mate)):
            push(
                part_ref.at[band(q), span(d)], got_mate.at[d, k],
                send_a.at[d, k], recv_a.at[d, k], (mate, f),
            )
    loads = [
        pltpu.make_async_copy(window_hbm, window_ref, load_sem.at[0]),
        pltpu.make_async_copy(token_hbm, token_ref, load_sem.at[1]),
    ]
    for load in loads:
        load.start()
    for d in range(lines):
        arrive(got_mate.at[d, 0], send_a.at[d, 0], recv_a.at[d, 0])
        sum_x[d] = (
            part_ref[band(across), span(d)].astype(f32) + got_mate[d, 0].astype(f32)
        ).astype(bf16)
        push(sum_x.at[d], got_x.at[d], send_x.at[d], recv_x.at[d], (across, f))
    for load in loads:
        load.wait()
    gain_row[...] = jnp.zeros_like(gain_row)
    height, width = product.shape
    tile = width // 4

    def store(i):
        own = pl.ds(pl.multiple_of(i * height, height), height)
        return pltpu.make_async_copy(grad_ref.at[own], grad_hbm.at[own], store_sem.at[i])

    def token_block(i, carry):
        own = pl.ds(pl.multiple_of(i * height, height), height)
        inv = inv_ref[own, :]
        dots = jnp.zeros((height, 1), f32)
        for c in range(4):
            cols = slice(c * tile, (c + 1) * tile)
            grad = jnp.dot(logit_ref[own, :], window_ref[:, cols], preferred_element_type=f32)
            wide = token_ref[own, cols].astype(f32)
            gain_row[:, cols] += jnp.sum(grad * wide * inv, axis=0, keepdims=True)
            scaled = grad * norm_ref[:, cols]
            product[:, cols] = scaled
            dots = dots + jnp.sum(scaled * wide, axis=1, keepdims=True)
        factor = inv * inv * inv * (dots / width)
        for c in range(4):
            cols = slice(c * tile, (c + 1) * tile)
            wide = token_ref[own, cols].astype(f32)
            grad_ref[own, cols] = (inv * product[:, cols] - wide * factor).astype(bf16)
        store(i).start()
        return carry

    blocks = token_ref.shape[0] // height
    lax.fori_loop(0, blocks, token_block, 0)
    for g in range(n):
        gain_ref[g] = gain_row[:, g * columns : (g + 1) * columns]
    for d in range(1, n):
        device = peers[d - 1]
        push(gain_ref.at[device[1]], got_gain.at[d], gsend.at[d], grecv.at[d], device)

    def gathered(d, h):
        return (
            part_ref[band(s), half_span(d, h)].astype(f32)
            + got_mate[d, 1, :, half(h)].astype(f32)
            + got_x[d, :, half(h)].astype(f32)
        )

    def finish(d):
        arrive(got_y.at[d], send_y.at[d], recv_y.at[d])
        value = gathered(d, b) + got_y[d].astype(f32)
        if d < lines - 1:
            sum_z[d] = value.astype(bf16)
            push(sum_z.at[d], got_z.at[d], send_z.at[d], recv_z.at[d], (s, 2 * chunk[d] + b))
        return value

    for d in range(lines):
        arrive(got_mate.at[d, 1], send_a.at[d, 1], recv_a.at[d, 1])
        arrive(got_x.at[d], send_x.at[d], recv_x.at[d])
        sum_y[d] = gathered(d, 1 - b).astype(bf16)
        push(sum_y.at[d], got_y.at[d], send_y.at[d], recv_y.at[d], (s, 2 * a + 1 - b))
        if d > 0:
            finish(d - 1)
    total = gain_ref[f]
    for d in range(1, n):
        arrive(got_gain.at[d], gsend.at[d], grecv.at[d])
        total = total + got_gain[d]
    gain_sum[...] = total
    for d in range(1, 4):
        push(gain_sum, got_sum.at[d], ssend.at[d], srecv.at[d], sections[d - 1])
    value = finish(lines - 1)
    for d in range(lines - 1):
        arrive(got_z.at[d], send_z.at[d], recv_z.at[d])
        value = value + got_z[d].astype(f32)
    final[...] = value.astype(bf16)
    push(final, out_ref.at[band(s)], send_o.at[0], recv_o.at[0], (across, f))
    push(final, out_ref.at[band(s)], send_o.at[1], recv_o.at[1], (mate, f))
    out_ref[band(s), :] = value.astype(bf16)
    for d in range(1, 4):
        arrive(got_sum.at[d], ssend.at[d], srecv.at[d])
    gain_out[...] = gain_sum[...] + got_sum[1] + got_sum[2] + got_sum[3]
    arrive(out_ref.at[band(across)], send_o.at[0], recv_o.at[0])
    push(
        out_ref.at[band(across)], out_ref.at[band(across)],
        send_o.at[2], recv_o.at[2], (mate, f),
    )
    arrive(out_ref.at[band(mate)], send_o.at[1], recv_o.at[1])
    arrive(out_ref.at[band(diagonal)], send_o.at[2], recv_o.at[2])
    for i in range(blocks):
        store(i).wait()
    for copy in sent:
        copy.wait_send()


def reduce_head(part, grad_logits, window, tokens, inv_rms, gain, n):
    terms, width = part.shape
    count = tokens.shape[0]
    rows, columns, lines = terms // 4, width // n, n // 2
    sems = [pltpu.SemaphoreType.DMA((lines, 2))] * 2 + [pltpu.SemaphoreType.DMA((lines,))] * 6
    sems += [pltpu.SemaphoreType.DMA((3,))] * 2 + [pltpu.SemaphoreType.DMA((n,))] * 2
    sems += [pltpu.SemaphoreType.DMA((4,))] * 2
    return pl.pallas_call(
        lambda *refs: reduce_kernel(n, *refs),
        name="reduce_head",
        out_shape=(
            jax.ShapeDtypeStruct((terms, columns), bf16),
            jax.ShapeDtypeStruct((1, columns), f32),
            jax.ShapeDtypeStruct(tokens.shape, bf16),
        ),
        in_specs=[VMEM, VMEM, ANY, ANY, VMEM, VMEM],
        out_specs=(VMEM, VMEM, ANY),
        scratch_shapes=[
            pltpu.VMEM((terms, width), bf16),
            pltpu.VMEM((count, width), bf16),
            pltpu.VMEM((count, width), bf16),
            pltpu.VMEM((LEN // 2, width), f32),
            pltpu.VMEM((1, width), f32),
            pltpu.VMEM((n, 1, columns), f32),
            pltpu.SemaphoreType.DMA((2,)),
            pltpu.SemaphoreType.DMA((2 * count // LEN,)),
            pltpu.VMEM((lines, 2, rows, 2 * columns), bf16),
            pltpu.VMEM((lines, rows, 2 * columns), bf16),
            pltpu.VMEM((lines, rows, 2 * columns), bf16),
            pltpu.VMEM((lines, rows, columns), bf16),
            pltpu.VMEM((lines, rows, columns), bf16),
            pltpu.VMEM((lines, rows, columns), bf16),
            pltpu.VMEM((lines, rows, columns), bf16),
            pltpu.VMEM((rows, columns), bf16),
            pltpu.VMEM((n, 1, columns), f32),
            pltpu.VMEM((1, columns), f32),
            pltpu.VMEM((4, 1, columns), f32),
        ]
        + sems,
        compiler_params=pltpu.CompilerParams(
            collective_id=2, has_side_effects=True, vmem_limit_bytes=60 << 20
        ),
    )(part, grad_logits, window, tokens, inv_rms, gain)


def local(produced, lengths, active, window_blocks, triplets, teacher, norm_gain, head):
    sections, shards = lax.axis_size("section"), lax.axis_size("fsdp")
    places = triplets[0] // SEQ_DEV * PAD + triplets[0] % SEQ_DEV
    group_data = jnp.concatenate([places.astype(jnp.float32), teacher[0][:, None]], axis=1)
    group_data = passed_along(group_data, "section", -1)
    columns = head.shape[1]
    own_blocks = U // sections
    block_ids = lax.dynamic_slice(
        window_blocks, (lax.axis_index("section") * own_blocks,), (own_blocks,)
    )
    local_rows = head.reshape(head.shape[0] // BLOCK, BLOCK, columns)[block_ids].reshape(
        own_blocks * BLOCK, columns
    )
    gain_own = norm_gain.astype(jnp.float32)[None, :]
    window, gains = gather_window(local_rows, gain_own, shards)
    gain32 = gains.reshape(D)
    tokens = produced.reshape(SEQ_DEV * LEN, D)
    widened = tokens.astype(jnp.float32)
    inv_rms = lax.rsqrt(jnp.mean(widened * widened, axis=1, keepdims=True) + eps)
    normed = (widened * inv_rms * gain32).astype(jnp.bfloat16)
    seq_len_row = lengths[0]
    slot_table = active[0]
    position = jnp.arange(LEN, dtype=jnp.int32)
    weight = (position[None, :] < seq_len_row[:, None]).astype(jnp.float32) / seq_len_row[
        :, None
    ].astype(jnp.float32)
    slot_range = jnp.arange(U, dtype=jnp.int32)
    onehot = (slot_table[:, :, None] == slot_range[None, None, :]).astype(jnp.float32)
    chosen = jnp.sum(onehot, axis=1)
    spread = jnp.repeat(chosen, BLOCK, axis=1)
    logits = jnp.einsum("td,jd->tj", normed, window, preferred_element_type=jnp.float32)
    values, slopes = pool_terms(logits.reshape(SEQ_DEV, LEN, U * BLOCK))
    pooled = jnp.sum(weight[:, :, None] * values, axis=1) * spread
    padding = ((0, PAD - SEQ_DEV), (0, 0))
    grad_values, loss_row = pooled_grads(
        jnp.pad(pooled, padding), group_data, jnp.pad(spread, padding), shards
    )
    grad_values = grad_values[:SEQ_DEV]
    loss_value = passed_along(loss_row[0, :1], "section", 1)
    grad_logits = (weight[:, :, None] * grad_values[:, None, :] * slopes).astype(jnp.bfloat16)
    grad_logits = grad_logits.reshape(SEQ_DEV * LEN, U * BLOCK)
    head_part = jnp.einsum(
        "tj,td->jd", grad_logits, normed, preferred_element_type=jnp.float32
    ).astype(jnp.bfloat16)
    head_piece, gain_piece, grad_tokens = reduce_head(
        head_part, grad_logits, window, tokens, inv_rms, gain32[None, :], shards
    )
    outgoing = grad_tokens.reshape(1, SEQ_DEV, LEN, D)
    head_piece = head_piece.astype(jnp.float32)
    gain_piece = gain_piece.reshape(columns)
    return (loss_value, outgoing, head_piece, gain_piece)


def solution(mesh):
    return jax.shard_map(
        local,
        mesh=mesh,
        in_specs=(
            P("section", "fsdp", None, None),
            P("section", "fsdp"),
            P("section", "fsdp", None),
            P(),
            P("section", None, None),
            P("section", None),
            P("fsdp"),
            P(None, "fsdp"),
        ),
        out_specs=(P("section"), P("section", "fsdp", None, None), P(None, "fsdp"), P("fsdp")),
        check_vma=False,
    )
```

```python
import jax
import jax.numpy as jnp
from jax import lax
from jax.experimental import pallas as pl
from jax.experimental.pallas import tpu as pltpu
from jax.sharding import PartitionSpec as P

D = 4096
BLOCK = 128
U = 8
LEN = 256
SEQ_DEV = 3


eps = 1e-05
loss_scale = 256.0


def passed_along(block, axis, distance):
    devices = range(lax.axis_size(axis))
    route = [((i - distance) % len(devices), i) for i in devices]
    return lax.ppermute(block, axis, route)


def pool_terms(logits):
    smooth = jax.nn.softplus(logits)
    return (jnp.log1p(smooth), jax.nn.sigmoid(logits) / (1.0 + smooth))


MESH = pl.DeviceIdType.MESH
VMEM = pl.BlockSpec(memory_space=pltpu.VMEM)
ANY = pl.BlockSpec(memory_space=pl.ANY)
bf16, f32 = jnp.bfloat16, jnp.float32


def place():
    s, f = lax.axis_index("section"), lax.axis_index("fsdp")
    mate = s + 1 - 2 * lax.rem(s, 2)
    across = lax.rem(s + 2, 4)
    return s, f, mate, across


def greet(others):
    barrier = pltpu.get_barrier_semaphore()
    for device in others:
        pl.semaphore_signal(barrier, inc=1, device_id=device, device_id_type=MESH)
    pl.semaphore_wait(barrier, len(others))


def remote(src, dst, send, recv, device):
    return pltpu.make_async_remote_copy(
        src_ref=src,
        dst_ref=dst,
        send_sem=send,
        recv_sem=recv,
        device_id=device,
        device_id_type=MESH,
    )


def gather_kernel(
    n, piece_ref, gain_ref, token_hbm, window_ref, gains_ref, normed_ref, inv_ref, logits_ref,
    token_ref, quarter, send, recv, gsend, grecv, own_sem, token_sem, load_sem,
):
    s, f, mate, across = place()
    lines = n // 2
    a, b = lax.div(f, 2), lax.rem(f, 2)
    rows, columns = piece_ref.shape
    peers = [(s, lax.rem(f + d, n)) for d in range(1, n)]
    greet(peers + [(mate, f), (across, f)])
    sent = []

    def region(q, g):
        return window_ref.at[
            pl.ds(pl.multiple_of(q * rows, rows), rows),
            pl.ds(pl.multiple_of(g * columns, columns), columns),
        ]

    def push(src, q, g, index, device):
        copy = remote(src, region(q, g), send.at[index], recv.at[index], device)
        copy.start()
        sent.append(copy)

    def arrive(q, g, index):
        spot = region(q, g)
        remote(spot, spot, send.at[index], recv.at[index], (mate, f)).wait_recv()
        return spot

    side = lambda d: 2 * lax.rem(a - d + lines, lines) + b
    other = lambda d: 2 * lax.rem(a - d + lines, lines) + 1 - b
    to_y, to_x, to_mate, to_last = lines, 2 * lines, 4 * lines, 6 * lines

    def spread_out(src, g, d, half):
        push(src, s, g, to_x + half * lines + d, (across, f))
        push(src, s, g, to_mate + half * lines + d, (mate, f))

    for d in range(1, lines):
        push(piece_ref, s, f, d, (s, 2 * lax.rem(a + d, lines) + b))
    push(piece_ref, s, f, to_y, (s, 2 * a + 1 - b))
    spread_out(piece_ref, f, 0, 0)
    own = pltpu.make_async_copy(piece_ref, region(s, f), own_sem)
    own.start()
    gain_copies = []
    for d in range(1, n):
        copy = remote(gain_ref, gains_ref.at[f], gsend.at[d], grecv.at[d], peers[d - 1])
        copy.start()
        gain_copies.append(copy)
    gains_ref[f] = gain_ref[...]
    width = token_ref.shape[1]
    blocks = token_ref.shape[0] // LEN

    def rows_of(i):
        return pl.ds(pl.multiple_of(i * LEN, LEN), LEN)

    def measure_block(i, carry):
        squares = jnp.zeros((LEN, 1), f32)
        for g in range(n):
            wide = token_ref[rows_of(i), g * columns : (g + 1) * columns].astype(f32)
            squares = squares + jnp.sum(wide * wide, axis=1, keepdims=True)
        inv_ref[rows_of(i), :] = lax.rsqrt(squares / width + eps)
        return carry

    def norm_block(i, carry):
        inv = inv_ref[rows_of(i), :]
        for g in range(n):
            cols = slice(g * columns, (g + 1) * columns)
            wide = token_ref[rows_of(i), cols].astype(f32)
            normed_ref[rows_of(i), cols] = (wide * inv * gains_ref[g]).astype(bf16)
        return carry

    def load_quarter(q, k):
        band = window_ref.at[pl.ds(pl.multiple_of(q * rows, rows), rows)]
        load = pltpu.make_async_copy(band, quarter.at[k], load_sem.at[k])
        load.start()
        return load

    def logits_of(q, k, load):
        load.wait()

        def block(i, carry):
            logits_ref[rows_of(i), pl.ds(pl.multiple_of(q * rows, rows), rows)] = lax.dot_general(
                normed_ref[rows_of(i), :],
                quarter[k],
                (((1,), (1,)), ((), ())),
                preferred_element_type=f32,
            )
            return carry

        lax.fori_loop(0, blocks, block, 0)

    tokens = pltpu.make_async_copy(token_hbm, token_ref, token_sem)
    tokens.start()
    tokens.wait()
    lax.fori_loop(0, blocks, measure_block, 0)
    spread_out(arrive(s, other(0), to_y), other(0), 0, 1)
    for d in range(1, lines):
        spot = arrive(s, side(d), d)
        push(spot, s, side(d), to_y + d, (s, 2 * a + 1 - b))
        spread_out(spot, side(d), d, 0)
    for d in range(1, n):
        spot = gains_ref.at[lax.rem(f - d + n, n)]
        remote(spot, spot, gsend.at[d], grecv.at[d], peers[d - 1]).wait_recv()
    lax.fori_loop(0, blocks, norm_block, 0)
    for d in range(1, lines):
        spread_out(arrive(s, other(d), to_y + d), other(d), d, 1)
    order = [(0, 0), (0, 1)] + [(d, 0) for d in range(1, lines)] + [(d, 1) for d in range(1, lines)]
    name = lambda d, half: other(d) if half else side(d)
    mate_across = lax.rem(mate + 2, 4)
    own.wait()
    own_load = load_quarter(s, 0)
    for d, half in order:
        arrive(mate, name(d, half), to_mate + half * lines + d)
    mate_load = load_quarter(mate, 1)
    logits_of(s, 0, own_load)
    for k, (d, half) in enumerate(order):
        if k == len(order) // 2:
            logits_of(mate, 1, mate_load)
        spot = arrive(across, name(d, half), to_x + half * lines + d)
        push(spot, across, name(d, half), to_last + half * lines + d, (mate, f))
    logits_of(across, 2, load_quarter(across, 2))
    for d, half in order:
        arrive(mate_across, name(d, half), to_last + half * lines + d)
    logits_of(mate_across, 3, load_quarter(mate_across, 3))
    for copy in sent + gain_copies:
        copy.wait_send()


def gather_window(piece, gain, tokens, n):
    rows, columns = piece.shape
    tall, width = tokens.shape
    count = 8 * (n // 2)
    return pl.pallas_call(
        lambda *refs: gather_kernel(n, *refs),
        name="gather_window",
        out_shape=(
            jax.ShapeDtypeStruct((4 * rows, n * columns), bf16),
            jax.ShapeDtypeStruct((n, 1, columns), f32),
            jax.ShapeDtypeStruct((tall, width), bf16),
            jax.ShapeDtypeStruct((tall, 1), f32),
            jax.ShapeDtypeStruct((tall, 4 * rows), f32),
        ),
        in_specs=[VMEM, VMEM, ANY],
        out_specs=(ANY, VMEM, VMEM, VMEM, VMEM),
        scratch_shapes=[
            pltpu.VMEM((tall, width), bf16),
            pltpu.VMEM((4, rows, width), bf16),
            pltpu.SemaphoreType.DMA((count,)),
            pltpu.SemaphoreType.DMA((count,)),
            pltpu.SemaphoreType.DMA((n,)),
            pltpu.SemaphoreType.DMA((n,)),
            pltpu.SemaphoreType.DMA,
            pltpu.SemaphoreType.DMA,
            pltpu.SemaphoreType.DMA((4,)),
        ],
        compiler_params=pltpu.CompilerParams(
            collective_id=0, has_side_effects=True, vmem_limit_bytes=56 << 20
        ),
    )(piece, gain, tokens)


PAD = 8


def pick(hits, rows):
    return jnp.dot(hits, rows, precision=lax.Precision.HIGHEST, preferred_element_type=f32)


def pool_kernel(n, in_ref, group_ref, turned_ref, spread_ref, grad_ref, loss_ref, held, send, recv):
    s, f, _, _ = place()
    trips = group_ref.shape[0]
    peers = [(s, lax.rem(f + d, n)) for d in range(1, n)]
    greet(peers)
    copies = []
    for d in range(1, n):
        copy = remote(in_ref, held.at[f], send.at[d], recv.at[d], peers[d - 1])
        copy.start()
        copies.append(copy)
    held[f] = in_ref[...]
    names = lax.broadcasted_iota(jnp.int32, (trips, n * PAD), 1).astype(f32)
    group = group_ref[...]
    hits = [(names == group[:, k : k + 1]).astype(f32) for k in range(3)]
    own = (lax.broadcasted_iota(jnp.int32, (PAD, trips), 0) + f * PAD).astype(f32)
    turned = turned_ref[...]
    own_hits = [(own == turned[k : k + 1, :]).astype(f32) for k in range(3)]
    for d in range(1, n):
        spot = held.at[lax.rem(f - d + n, n)]
        remote(spot, spot, send.at[d], recv.at[d], peers[d - 1]).wait_recv()
    rows = held[...].reshape(n * PAD, held.shape[2])
    query = pick(hits[0], rows)
    gap = pick(hits[1], rows) - pick(hits[2], rows)
    deviation = jnp.sum(query * gap, axis=1, keepdims=True) - group[:, 3:4]
    loss = jnp.sum(deviation * deviation, axis=0, keepdims=True) / trips
    loss_ref[...] = jnp.broadcast_to(loss, loss_ref.shape)
    grad_margin = loss_scale * 2.0 * deviation / trips
    grad = pick(own_hits[0], grad_margin * gap)
    grad = grad + pick(own_hits[1] - own_hits[2], grad_margin * query)
    grad_ref[...] = grad * spread_ref[...]
    for copy in copies:
        copy.wait_send()


def pooled_grads(pooled, group, spread, n):
    return pl.pallas_call(
        lambda *refs: pool_kernel(n, *refs),
        name="pooled_grads",
        out_shape=(
            jax.ShapeDtypeStruct(pooled.shape, f32),
            jax.ShapeDtypeStruct((1, 128), f32),
        ),
        in_specs=[VMEM] * 4,
        out_specs=(VMEM, VMEM),
        scratch_shapes=[
            pltpu.VMEM((n,) + pooled.shape, f32),
            pltpu.SemaphoreType.DMA((n,)),
            pltpu.SemaphoreType.DMA((n,)),
        ],
        compiler_params=pltpu.CompilerParams(collective_id=1, has_side_effects=True),
    )(pooled, group, group.T, spread)


def reduce_kernel(
    n, part_ref, logit_ref, window_hbm, token_hbm, inv_ref, norm_ref, out_ref, gain_out, grad_hbm,
    window_ref, token_ref, grad_ref, product, gain_row, gain_ref, load_sem, store_sem,
    got_mate, sum_x, got_x, sum_y, got_y, sum_z, got_z, final, got_gain, gain_sum, got_sum,
    send_a, recv_a, send_x, recv_x, send_y, recv_y, send_z, recv_z, send_o, recv_o,
    gsend, grecv, ssend, srecv,
):
    s, f, mate, across = place()
    lines = n // 2
    a, b = lax.div(f, 2), lax.rem(f, 2)
    rows, columns = final.shape
    diagonal = lax.rem(mate + 2, 4)
    peers = [(s, lax.rem(f + d, n)) for d in range(1, n)]
    sections = [(lax.rem(s + d, 4), f) for d in range(1, 4)]
    greet(peers + sections)
    sent = []

    def push(src, dst, send, recv, device):
        copy = remote(src, dst, send, recv, device)
        copy.start()
        sent.append(copy)

    def arrive(spot, send, recv):
        remote(spot, spot, send, recv, (mate, f)).wait_recv()

    chunk = [lax.rem(a + 1 + d, lines) for d in range(lines)]

    def band(q):
        return pl.ds(pl.multiple_of(q * rows, rows), rows)

    def span(d):
        return pl.ds(pl.multiple_of(chunk[d] * 2 * columns, 2 * columns), 2 * columns)

    def half_span(d, half):
        return pl.ds(
            pl.multiple_of((chunk[d] * 2 + half) * columns, columns), columns
        )

    def half(h):
        return pl.ds(pl.multiple_of(h * columns, columns), columns)

    for d in range(lines):
        for k, q in ((0, diagonal), (1, mate)):
            push(
                part_ref.at[band(q), span(d)], got_mate.at[d, k],
                send_a.at[d, k], recv_a.at[d, k], (mate, f),
            )
    loads = [
        pltpu.make_async_copy(window_hbm, window_ref, load_sem.at[0]),
        pltpu.make_async_copy(token_hbm, token_ref, load_sem.at[1]),
    ]
    for load in loads:
        load.start()
    for d in range(lines):
        arrive(got_mate.at[d, 0], send_a.at[d, 0], recv_a.at[d, 0])
        sum_x[d] = (
            part_ref[band(across), span(d)].astype(f32) + got_mate[d, 0].astype(f32)
        ).astype(bf16)
        push(sum_x.at[d], got_x.at[d], send_x.at[d], recv_x.at[d], (across, f))
    for load in loads:
        load.wait()
    gain_row[...] = jnp.zeros_like(gain_row)
    height, width = product.shape
    tile = width // 4

    def store(i):
        own = pl.ds(pl.multiple_of(i * height, height), height)
        return pltpu.make_async_copy(grad_ref.at[own], grad_hbm.at[own], store_sem.at[i])

    def token_block(i, carry):
        own = pl.ds(pl.multiple_of(i * height, height), height)
        inv = inv_ref[own, :]
        dots = jnp.zeros((height, 1), f32)
        for c in range(4):
            cols = slice(c * tile, (c + 1) * tile)
            grad = jnp.dot(logit_ref[own, :], window_ref[:, cols], preferred_element_type=f32)
            wide = token_ref[own, cols].astype(f32)
            gain_row[:, cols] += jnp.sum(grad * wide * inv, axis=0, keepdims=True)
            scaled = grad * norm_ref[:, cols]
            product[:, cols] = scaled
            dots = dots + jnp.sum(scaled * wide, axis=1, keepdims=True)
        factor = inv * inv * inv * (dots / width)
        for c in range(4):
            cols = slice(c * tile, (c + 1) * tile)
            wide = token_ref[own, cols].astype(f32)
            grad_ref[own, cols] = (inv * product[:, cols] - wide * factor).astype(bf16)
        store(i).start()
        return carry

    blocks = token_ref.shape[0] // height
    lax.fori_loop(0, blocks, token_block, 0)
    for g in range(n):
        gain_ref[g] = gain_row[:, g * columns : (g + 1) * columns]
    for d in range(1, n):
        device = peers[d - 1]
        push(gain_ref.at[device[1]], got_gain.at[d], gsend.at[d], grecv.at[d], device)

    def gathered(d, h):
        return (
            part_ref[band(s), half_span(d, h)].astype(f32)
            + got_mate[d, 1, :, half(h)].astype(f32)
            + got_x[d, :, half(h)].astype(f32)
        )

    def finish(d):
        arrive(got_y.at[d], send_y.at[d], recv_y.at[d])
        value = gathered(d, b) + got_y[d].astype(f32)
        if d < lines - 1:
            sum_z[d] = value.astype(bf16)
            push(sum_z.at[d], got_z.at[d], send_z.at[d], recv_z.at[d], (s, 2 * chunk[d] + b))
        return value

    for d in range(lines):
        arrive(got_mate.at[d, 1], send_a.at[d, 1], recv_a.at[d, 1])
        arrive(got_x.at[d], send_x.at[d], recv_x.at[d])
        sum_y[d] = gathered(d, 1 - b).astype(bf16)
        push(sum_y.at[d], got_y.at[d], send_y.at[d], recv_y.at[d], (s, 2 * a + 1 - b))
        if d > 0:
            finish(d - 1)
    total = gain_ref[f]
    for d in range(1, n):
        arrive(got_gain.at[d], gsend.at[d], grecv.at[d])
        total = total + got_gain[d]
    gain_sum[...] = total
    for d in range(1, 4):
        push(gain_sum, got_sum.at[d], ssend.at[d], srecv.at[d], sections[d - 1])
    value = finish(lines - 1)
    for d in range(lines - 1):
        arrive(got_z.at[d], send_z.at[d], recv_z.at[d])
        value = value + got_z[d].astype(f32)
    final[...] = value.astype(bf16)
    push(final, out_ref.at[band(s)], send_o.at[0], recv_o.at[0], (across, f))
    push(final, out_ref.at[band(s)], send_o.at[1], recv_o.at[1], (mate, f))
    out_ref[band(s), :] = value.astype(bf16)
    for d in range(1, 4):
        arrive(got_sum.at[d], ssend.at[d], srecv.at[d])
    gain_out[...] = gain_sum[...] + got_sum[1] + got_sum[2] + got_sum[3]
    arrive(out_ref.at[band(across)], send_o.at[0], recv_o.at[0])
    push(
        out_ref.at[band(across)], out_ref.at[band(across)],
        send_o.at[2], recv_o.at[2], (mate, f),
    )
    arrive(out_ref.at[band(mate)], send_o.at[1], recv_o.at[1])
    arrive(out_ref.at[band(diagonal)], send_o.at[2], recv_o.at[2])
    for i in range(blocks):
        store(i).wait()
    for copy in sent:
        copy.wait_send()


def reduce_head(part, grad_logits, window, tokens, inv_rms, gain, n):
    terms, width = part.shape
    count = tokens.shape[0]
    rows, columns, lines = terms // 4, width // n, n // 2
    sems = [pltpu.SemaphoreType.DMA((lines, 2))] * 2 + [pltpu.SemaphoreType.DMA((lines,))] * 6
    sems += [pltpu.SemaphoreType.DMA((3,))] * 2 + [pltpu.SemaphoreType.DMA((n,))] * 2
    sems += [pltpu.SemaphoreType.DMA((4,))] * 2
    return pl.pallas_call(
        lambda *refs: reduce_kernel(n, *refs),
        name="reduce_head",
        out_shape=(
            jax.ShapeDtypeStruct((terms, columns), bf16),
            jax.ShapeDtypeStruct((1, columns), f32),
            jax.ShapeDtypeStruct(tokens.shape, bf16),
        ),
        in_specs=[VMEM, VMEM, ANY, ANY, VMEM, VMEM],
        out_specs=(VMEM, VMEM, ANY),
        scratch_shapes=[
            pltpu.VMEM((terms, width), bf16),
            pltpu.VMEM((count, width), bf16),
            pltpu.VMEM((count, width), bf16),
            pltpu.VMEM((LEN // 2, width), f32),
            pltpu.VMEM((1, width), f32),
            pltpu.VMEM((n, 1, columns), f32),
            pltpu.SemaphoreType.DMA((2,)),
            pltpu.SemaphoreType.DMA((2 * count // LEN,)),
            pltpu.VMEM((lines, 2, rows, 2 * columns), bf16),
            pltpu.VMEM((lines, rows, 2 * columns), bf16),
            pltpu.VMEM((lines, rows, 2 * columns), bf16),
            pltpu.VMEM((lines, rows, columns), bf16),
            pltpu.VMEM((lines, rows, columns), bf16),
            pltpu.VMEM((lines, rows, columns), bf16),
            pltpu.VMEM((lines, rows, columns), bf16),
            pltpu.VMEM((rows, columns), bf16),
            pltpu.VMEM((n, 1, columns), f32),
            pltpu.VMEM((1, columns), f32),
            pltpu.VMEM((4, 1, columns), f32),
        ]
        + sems,
        compiler_params=pltpu.CompilerParams(
            collective_id=2, has_side_effects=True, vmem_limit_bytes=60 << 20
        ),
    )(part, grad_logits, window, tokens, inv_rms, gain)


def local(produced, lengths, active, window_blocks, triplets, teacher, norm_gain, head):
    sections, shards = lax.axis_size("section"), lax.axis_size("fsdp")
    places = triplets[0] // SEQ_DEV * PAD + triplets[0] % SEQ_DEV
    group_data = jnp.concatenate([places.astype(jnp.float32), teacher[0][:, None]], axis=1)
    group_data = passed_along(group_data, "section", -1)
    columns = head.shape[1]
    own_blocks = U // sections
    block_ids = lax.dynamic_slice(
        window_blocks, (lax.axis_index("section") * own_blocks,), (own_blocks,)
    )
    local_rows = head.reshape(head.shape[0] // BLOCK, BLOCK, columns)[block_ids].reshape(
        own_blocks * BLOCK, columns
    )
    gain_own = norm_gain.astype(jnp.float32)[None, :]
    tokens = produced.reshape(SEQ_DEV * LEN, D)
    window, gains, normed, inv_rms, logits = gather_window(local_rows, gain_own, tokens, shards)
    gain32 = gains.reshape(D)
    seq_len_row = lengths[0]
    slot_table = active[0]
    position = jnp.arange(LEN, dtype=jnp.int32)
    weight = (position[None, :] < seq_len_row[:, None]).astype(jnp.float32) / seq_len_row[
        :, None
    ].astype(jnp.float32)
    slot_range = jnp.arange(U, dtype=jnp.int32)
    onehot = (slot_table[:, :, None] == slot_range[None, None, :]).astype(jnp.float32)
    chosen = jnp.sum(onehot, axis=1)
    spread = jnp.repeat(chosen, BLOCK, axis=1)
    values, slopes = pool_terms(logits.reshape(SEQ_DEV, LEN, U * BLOCK))
    pooled = jnp.sum(weight[:, :, None] * values, axis=1) * spread
    padding = ((0, PAD - SEQ_DEV), (0, 0))
    grad_values, loss_row = pooled_grads(
        jnp.pad(pooled, padding), group_data, jnp.pad(spread, padding), shards
    )
    grad_values = grad_values[:SEQ_DEV]
    loss_value = passed_along(loss_row[0, :1], "section", 1)
    grad_logits = (weight[:, :, None] * grad_values[:, None, :] * slopes).astype(jnp.bfloat16)
    grad_logits = grad_logits.reshape(SEQ_DEV * LEN, U * BLOCK)
    head_part = jnp.einsum(
        "tj,td->jd", grad_logits, normed, preferred_element_type=jnp.float32
    ).astype(jnp.bfloat16)
    head_piece, gain_piece, grad_tokens = reduce_head(
        head_part, grad_logits, window, tokens, inv_rms, gain32[None, :], shards
    )
    outgoing = grad_tokens.reshape(1, SEQ_DEV, LEN, D)
    head_piece = head_piece.astype(jnp.float32)
    gain_piece = gain_piece.reshape(columns)
    return (loss_value, outgoing, head_piece, gain_piece)


def solution(mesh):
    return jax.shard_map(
        local,
        mesh=mesh,
        in_specs=(
            P("section", "fsdp", None, None),
            P("section", "fsdp"),
            P("section", "fsdp", None),
            P(),
            P("section", None, None),
            P("section", None),
            P("fsdp"),
            P(None, "fsdp"),
        ),
        out_specs=(P("section"), P("section", "fsdp", None, None), P(None, "fsdp"), P("fsdp")),
        check_vma=False,
    )
```
